32 devices in a mesh: groups: 2 (over x), seq: 16 (over z, y, core).
Axes of the slice: x: 2, y: 2, z: 4, core: 2. Of those that a mesh axis runs over, the one named last changes fastest.
Arguments:
- queries: bfloat16 [1024, 4096], P(('groups', 'seq')), parts along dimension 0, may hold values from -10 to 10
- visual_keys: bfloat16 [16384, 512], P(('groups', 'seq')), parts along dimension 0, may hold values from -6 to 6
- hidden: bfloat16 [16384, 8192], P(('groups', 'seq')), parts along dimension 0, may hold values from -6 to 6
- keep_count: int32 [32], P(('groups', 'seq')), parts along dimension 0, may hold values from 0 to 512, as said below
- keep_index: int32 [16384], P(('groups', 'seq')), parts along dimension 0, may hold values from 0 to 511, as said below
- norm_gain: float32 [8192], replicated, may hold values from 0.25 to 1.75
- kv_weight: bfloat16 [8192, 1024], replicated, may hold values from -0.0625 to 0.0625
- kv_bias: float32 [1024], replicated, may hold values from -3 to 3
Outputs:
- importance: float32 [16384], P(('groups', 'seq')), parts along dimension 0
- layer_kv: bfloat16 [8192, 1024], P(('groups', 'seq')), parts along dimension 0
The draws below stay inside these ranges and needn't reach their ends.
There are 2 independent parts, one for each index of `groups`. The reference program is written for one: setup_inputs(seed, part) draws one part's arguments, and reference() takes and returns one part's arrays. A program takes and returns all parts, laid end to end along the dimension named above; an argument that names none is the same for every part. Nothing has to cross between parts.
Inputs may be any that keep to these rules, and one draw needn't show every extreme that they name: keep_count sums to 16 * 256 over one part; some device keeps all its rows and some none. `keep_index`: each device's block of 512 entries lists first its kept rows, distinct and ascending, as many as its count, then its other rows; entries are row numbers within the device's block.
All inputs are finite; a program needn't handle non-finite values.
Results may differ from the reference program's by a relative error of at most 0.0046.
Values may be sent and summed in bfloat16 or wider, within the bound.
A program may use at most 192 MiB of HBM per device.

```python
import jax
import jax.numpy as jnp
from jax import lax

D = 8192
H = 32
KVH = 4
HD = 128
NT = 512
V_DEV = 512
NV = 8192
KEEP_DEV = 256
N_SEQ = 16


def align_plan(key):
    half_signs = jnp.where(jax.random.uniform(jax.random.fold_in(key, 11), (KVH, 8, HD // 2)) < 0.5, 1.0, -1.0).astype(jnp.float32)
    pattern = jnp.stack([half_signs, -half_signs], axis=-1).reshape(KVH, 8, HD)
    key_span = NV // 8
    position = jnp.arange(8, dtype=jnp.int32)[None, :]
    heads_col = jnp.arange(KVH, dtype=jnp.int32)[:, None]
    key_offset = jax.random.randint(jax.random.fold_in(key, 12), (KVH, 8), 0, key_span - 1).astype(jnp.int32)
    key_rows = (position * key_span + key_offset).astype(jnp.int32)
    query_offset = jax.random.randint(jax.random.fold_in(key, 13), (KVH, 8), 0, NT // 32).astype(jnp.int32)
    query_rows = (position * (NT // 8) + 4 * query_offset + (position + heads_col) % 4).astype(jnp.int32)
    strength_table = jnp.array([4.5, 7.0, 10.0, 4.5, 10.0, 7.0, 4.5, 10.0], jnp.float32)
    strength = jnp.take(strength_table, (position + heads_col) % 8)
    return (pattern, key_rows, query_rows, strength)


def draw_queries(key, part):
    coarse = jnp.clip(2.5 * jax.random.normal(jax.random.fold_in(key, 1), (NT, H * HD // 2), jnp.float32), -8.5, 8.5)
    fine_noise = jnp.clip(0.5 * jax.random.normal(jax.random.fold_in(key, 3), (NT, H * HD), jnp.float32), -1.5, 1.5)
    values_base = jnp.repeat(coarse, 2, axis=1) + fine_noise
    pattern, key_rows, query_rows, strength = align_plan(key)
    group_size = H // KVH
    for kv_head in range(KVH):
        block = jnp.tile(strength[kv_head][:, None] * pattern[kv_head], (1, group_size))
        first_col = kv_head * group_size * HD
        values_base = values_base.at[query_rows[kv_head], first_col:first_col + group_size * HD].set(block)
    return values_base.astype(jnp.bfloat16)


def draw_visual_keys(key, part):
    values_base = jnp.clip(jax.random.normal(jax.random.fold_in(key, 2), (NV, KVH * HD), jnp.float32), -4.0, 4.0)
    pattern, key_rows, query_rows, strength = align_plan(key)
    for kv_head in range(KVH):
        leading = 6.0 * pattern[kv_head]
        cut_share = 2.0 * jnp.sqrt(jnp.float32(HD)) / (6.0 * strength[kv_head])
        runner = leading.at[:, 0].multiply(1.0 - cut_share)
        first_col = kv_head * HD
        values_base = values_base.at[key_rows[kv_head], first_col:first_col + HD].set(leading)
        values_base = values_base.at[key_rows[kv_head] + 1, first_col:first_col + HD].set(runner)
    return values_base.astype(jnp.bfloat16)


def keep_plan(key):
    pairing = jax.random.permutation(jax.random.fold_in(key, 21), N_SEQ)
    amount = jax.random.randint(jax.random.fold_in(key, 22), (N_SEQ // 2,), 0, KEEP_DEV + 1)
    amount = amount.at[0].set(KEEP_DEV)
    change = jnp.zeros((N_SEQ,), jnp.int32).at[pairing[0::2]].set(amount).at[pairing[1::2]].set(-amount)
    return (KEEP_DEV + change).astype(jnp.int32)


def draw_keep_count(key, part):
    return keep_plan(key)


def draw_keep_index(key, part):
    counts = keep_plan(key)
    shuffle_keys = jax.random.split(jax.random.fold_in(key, 31), N_SEQ)
    shuffled = jax.vmap(lambda sub_key: jax.random.permutation(sub_key, V_DEV))(shuffle_keys)
    inverse = jnp.argsort(shuffled, axis=1)
    chosen = (inverse < counts[:, None]).astype(jnp.int32)
    listing = jnp.argsort(1 - chosen, axis=1, stable=True)
    return listing.reshape(-1).astype(jnp.int32)


def block_levels(key, extent, pieces, smallest, high):
    loudness, own = 1.0, jax.random.fold_in(key, 6)
    for dim, shards_of in pieces:
        draws = jnp.exp(jax.random.uniform(jax.random.fold_in(own, dim), (shards_of,), jnp.float32, smallest / len(pieces), high / len(pieces)))
        loudness = loudness * jnp.repeat(draws, extent[dim] // shards_of).reshape([-1 if axis == dim else 1 for axis in range(len(extent))])
    return loudness


def bell_draw(stream_key, shape, scale, reach, cuts=(), kind=jnp.bfloat16):
    level = block_levels(stream_key, shape, cuts, -0.22, 0.18) if cuts else 1.0
    result = jax.random.normal(stream_key, shape, jnp.float32) * scale * level
    return jnp.minimum(jnp.maximum(result, -reach), reach).astype(kind)


def setup_inputs(seed: int = 0, part: int = 0) -> dict:
    seeds = jax.random.split(jax.random.key(seed), 9)
    part_splits = jax.random.split(jax.random.fold_in(seeds[8], part), 9)
    return {
        "queries": draw_queries(jax.random.fold_in(jax.random.fold_in(seeds[8], part), 71), part),
        "visual_keys": draw_visual_keys(jax.random.fold_in(jax.random.fold_in(seeds[8], part), 71), part),
        "hidden": bell_draw(part_splits[2], (NV, D), 1.0, 6.0, ((0, 16),)),
        "keep_count": draw_keep_count(jax.random.fold_in(jax.random.fold_in(seeds[8], part), 71), part),
        "keep_index": draw_keep_index(jax.random.fold_in(jax.random.fold_in(seeds[8], part), 71), part),
        "norm_gain": jnp.clip(1.0 + 0.15 * jax.random.normal(seeds[5], (D,), jnp.float32), 0.25, 1.75),
        "kv_weight": bell_draw(seeds[6], (D, 2 * KVH * HD), D ** -0.5, 0.0625),
        "kv_bias": bell_draw(seeds[7], (2 * KVH * HD,), 0.5, 3.0, (), jnp.float32),
    }


def reference(queries, visual_keys, hidden, keep_count, keep_index, norm_gain, kv_weight, kv_bias):
    group_size = H // KVH
    query_heads = jnp.moveaxis(queries.astype(jnp.float32).reshape(NT, KVH, group_size, HD), 1, 0)
    key_heads = jnp.moveaxis(visual_keys.astype(jnp.float32).reshape(NV, KVH, HD), 1, 0)

    def per_head(head_pair):
        query_one, key_one = head_pair
        scores = jnp.einsum('tgd,vd->gtv', query_one, key_one) * HD ** (-0.5)
        row_top = lax.optimization_barrier(jnp.max(scores, axis=-1, keepdims=True))
        probability = jnp.exp(scores - row_top)
        probability = probability / lax.optimization_barrier(jnp.sum(probability, axis=-1, keepdims=True))
        return lax.optimization_barrier(jnp.sum(probability, axis=(0, 1)))
    columns = lax.map(per_head, (query_heads, key_heads))
    importance = lax.optimization_barrier(jnp.sum(columns, axis=0)) * (NV / (H * NT))
    counts = keep_count.astype(jnp.int32)
    run_ends = jnp.cumsum(counts).astype(jnp.int32)
    starts = (run_ends - counts).astype(jnp.int32)
    out_rows = jnp.arange(N_SEQ * KEEP_DEV, dtype=jnp.int32)
    owner_of = out_rows // KEEP_DEV
    slot_of = out_rows % KEEP_DEV
    rank_of = slot_of * N_SEQ + owner_of
    source = lax.optimization_barrier(jnp.sum((run_ends[None, :] <= rank_of[:, None]).astype(jnp.int32), axis=1)).astype(jnp.int32)
    within = (rank_of - starts[source]).astype(jnp.int32)
    local_row = keep_index[source * V_DEV + within].astype(jnp.int32)
    row_block = jnp.take(hidden, source * V_DEV + local_row, axis=0)
    values = row_block.astype(jnp.float32)
    mean_sq = lax.optimization_barrier(jnp.mean(values * values, axis=-1, keepdims=True))
    normed = (values * lax.rsqrt(mean_sq + 1e-06) * norm_gain).astype(jnp.bfloat16)
    layer_kv = (jnp.dot(normed, kv_weight, preferred_element_type=jnp.float32) + kv_bias).astype(jnp.bfloat16)
    return (importance, layer_kv)
```

```python
import functools

import jax
import jax.numpy as jnp
from jax import lax
from jax.experimental import pallas as pl
from jax.experimental.pallas import tpu as pltpu
from jax.sharding import PartitionSpec as P

HD = 128
EPS = 1e-6
CH = 128
KSTEP = 1024
MESH = pl.DeviceIdType.MESH
NT_DIMS = (((1,), (1,)), ((), ()))
LOG2E = 1.4426950408889634


def body(
    n, kvh, q_hbm, k_hbm, h_hbm, cnt_hbm, idx_ref, gain_ref, w_hbm, bias_ref,
    imp_ref, kv_ref,
    qbuf, kbuf, hid, wbuf, cnt, ssq, acc, proj, picked, rbuf, pbuf, mstat, lstat,
    lsend, lbuf, isend, ibuf,
    h_sem, w_sem, loc_sem, q_s, q_r, k_s, k_r, c_s, c_r, v_s, v_r, l_s, l_r, i_s, i_r,
):
    me = lax.axis_index("seq")
    planes = n // kvh
    head = lax.rem(me, kvh)
    plane = me // kvh
    rows, tq = h_hbm.shape[0], q_hbm.shape[0]
    width = h_hbm.shape[1]
    steps = width // KSTEP
    hw = q_hbm.shape[1] // kvh
    group = hw // HD
    nrow = group * tq
    cap = rows // n
    shift, cap_shift = n.bit_length() - 1, cap.bit_length() - 1
    keep = kv_ref.shape[0]
    nch = kvh * rows // CH
    scale = HD**-0.5 * LOG2E

    def h_copy(k):
        return pltpu.make_async_copy(
            h_hbm.at[:, pl.ds(pl.multiple_of(k * KSTEP, KSTEP), KSTEP)], hid.at[k], h_sem.at[k]
        )

    def w_copy(k):
        return pltpu.make_async_copy(
            w_hbm.at[pl.ds(pl.multiple_of(k * KSTEP, KSTEP), KSTEP), :], wbuf.at[k], w_sem.at[k]
        )

    def remote(src, dst, ssem, rsem, peer):
        return pltpu.make_async_remote_copy(
            src_ref=src, dst_ref=dst, send_sem=ssem, recv_sem=rsem,
            device_id={"seq": peer}, device_id_type=MESH,
        )

    def q_src(t):
        return q_hbm.at[:, pl.ds(pl.multiple_of(lax.rem(t, kvh) * hw, hw), hw)]

    def k_src(t):
        return k_hbm.at[:, pl.ds(pl.multiple_of(t * HD, HD), HD)]

    for k in range(steps):
        h_copy(k).start()
    for k in range(steps):
        w_copy(k).start()
    own = [
        pltpu.make_async_copy(q_src(me), qbuf.at[me], loc_sem.at[0]),
        pltpu.make_async_copy(k_src(head), kbuf.at[head], loc_sem.at[1]),
        pltpu.make_async_copy(cnt_hbm, cnt.at[me], loc_sem.at[2]),
    ]
    for c in own:
        c.start()

    bar = pltpu.get_barrier_semaphore()

    @pl.loop(1, n)
    def _(d):
        pl.semaphore_signal(bar, inc=1, device_id={"seq": lax.rem(me + d, n)}, device_id_type=MESH)

    pl.semaphore_wait(bar, n - 1)

    def c_copy(d):
        t = lax.rem(me + d, n)
        return remote(cnt_hbm, cnt.at[me], c_s.at[d], c_r.at[me], t)

    def q_copy(d):
        t = lax.rem(me + d, n)
        return remote(q_src(t), qbuf.at[me], q_s.at[d], q_r.at[me], t)

    def k_copy(d):
        t = lax.rem(head + d, kvh)
        return remote(k_src(t), kbuf.at[head], k_s.at[d], k_r.at[head], plane * kvh + t)

    def v_copy(d):
        t = lax.rem(me + d, n)
        return remote(picked.at[t], rbuf.at[me], v_s.at[d], v_r.at[me], t)

    def l_copy(d):
        t = lax.rem(plane + d, planes)
        return remote(lsend, lbuf.at[plane], l_s.at[d], l_r.at[plane], t * kvh + head)

    def i_copy(d):
        t = lax.rem(head + d, kvh)
        return remote(isend.at[t], ibuf.at[head], i_s.at[d], i_r.at[head], plane * kvh + t)

    def arrived(src, dst, ssem, rsem):
        remote(src, dst, ssem, rsem, lax.rem(me + 1, n)).wait_recv()

    @pl.loop(1, n)
    def _(d):
        c_copy(d).start()

    for d in range(1, kvh):
        k_copy(d).start()

    @pl.loop(1, n)
    def _(d):
        q_copy(d).start()

    ssq[...] = jnp.zeros_like(ssq)

    @pl.loop(0, steps)
    def _(k):
        h_copy(k).wait()
        x = hid[k].astype(jnp.float32)
        x = x * x
        part = x[:, :128]
        for j in range(1, KSTEP // 128):
            part += x[:, j * 128 : (j + 1) * 128]
        ssq[...] += part

    inv = lax.rsqrt(jnp.sum(ssq[...], axis=1, keepdims=True) / width + EPS)
    ssq[...] = jnp.broadcast_to(inv, ssq.shape)
    acc[...] = jnp.broadcast_to(bias_ref[...], acc.shape)

    @pl.loop(0, steps)
    def _(k):
        w_copy(k).wait()
        g = gain_ref[:, pl.ds(pl.multiple_of(k * KSTEP, KSTEP), KSTEP)]
        normed = (hid[k].astype(jnp.float32) * ssq[:, 0:1] * g).astype(jnp.bfloat16)
        acc[...] += jnp.dot(normed, wbuf[k], preferred_element_type=jnp.float32)

    proj[...] = acc[...].astype(jnp.bfloat16)

    own[2].wait()

    @pl.loop(1, n)
    def _(d):
        s = lax.rem(me + d, n)
        arrived(cnt_hbm, cnt.at[s], c_s.at[d], c_r.at[s])

    lanes = lax.broadcasted_iota(jnp.int32, (1, rows), 1)
    source = lax.shift_right_logical(lanes, cap_shift)
    run = jnp.zeros((1, rows), jnp.int32)
    start_of = jnp.zeros((1, rows), jnp.int32)
    count_of = jnp.zeros((1, rows), jnp.int32)
    my_start = jnp.zeros((1, rows), jnp.int32)
    for s in range(n):
        c = cnt[s, 0:1, :]
        start_of = jnp.where(source == s, run, start_of)
        count_of = jnp.where(source == s, c, count_of)
        my_start = my_start + jnp.where(s < me, c, 0)
        run = run + c

    row_id = lax.broadcasted_iota(jnp.int32, (rows, rows), 0)
    lane_id = lax.broadcasted_iota(jnp.int32, (rows, rows), 1)
    is_row = jnp.where(row_id == idx_ref[...], 1.0, 0.0).T.astype(jnp.bfloat16)
    kept = jnp.dot(is_row, proj[...], preferred_element_type=jnp.float32).astype(jnp.bfloat16)
    owner = lax.shift_right_logical(row_id, cap_shift)
    column = jnp.bitwise_and(row_id, cap - 1)
    pos = jnp.bitwise_and(owner - my_start, n - 1) + column * n
    is_pos = jnp.where(pos == lane_id, 1.0, 0.0).astype(jnp.bfloat16)
    out = jnp.dot(is_pos, kept, preferred_element_type=jnp.float32).astype(jnp.bfloat16)
    picked[...] = out.reshape(picked.shape)

    @pl.loop(1, n)
    def _(d):
        v_copy(d).start()

    own_v = pltpu.make_async_copy(picked.at[me], rbuf.at[me], loc_sem.at[3])
    own_v.start()

    own[0].wait()
    own[1].wait()
    for d in range(1, kvh):
        s = lax.rem(head + d, kvh)
        arrived(k_src(s), kbuf.at[s], k_s.at[d], k_r.at[s])

    def score(s):
        q = jnp.concatenate([qbuf[s, :, g * HD : (g + 1) * HD] for g in range(group)], axis=0)
        for c in range(nch):
            j, part = divmod(c * CH, rows)
            keys = kbuf[j, part : part + CH, :]
            t = lax.dot_general(keys, q, NT_DIMS, preferred_element_type=jnp.float32)
            top = jnp.max(t, axis=0, keepdims=True)
            p = jnp.exp2((t - top) * scale)
            mstat[s, c : c + 1, :] = top * scale
            lstat[s, c : c + 1, :] = jnp.sum(p, axis=0, keepdims=True)
            pbuf[s, c] = p.astype(jnp.bfloat16)

    @pl.loop(0, n)
    def _(d):
        s = lax.rem(me + d, n)

        @pl.when(d > 0)
        def _():
            arrived(q_src(s), qbuf.at[s], q_s.at[d], q_r.at[s])

        score(s)

    for s in range(n):
        m = mstat[s]
        top = jnp.max(m, axis=0, keepdims=True)
        total = jnp.sum(lstat[s] * jnp.exp2(m - top), axis=0, keepdims=True)
        lsend[s : s + 1, :] = top + jnp.log2(total)
    for d in range(1, planes):
        l_copy(d).start()
    for d in range(1, planes):
        s = lax.rem(plane + d, planes)
        arrived(lsend, lbuf.at[s], l_s.at[d], l_r.at[s])
    lbuf[plane] = lsend[...]
    lse = lbuf[...]
    top = jnp.max(lse, axis=0)
    lse = top + jnp.log2(jnp.sum(jnp.exp2(lse - top[None]), axis=0))
    for s in range(n):
        mstat[s] = jnp.exp2(mstat[s] - lse[s : s + 1, :])

    @pl.loop(0, kvh)
    def _(j):
        pieces = []
        for part in range(rows // CH):
            c = j * (rows // CH) + part

            def add(s, total):
                wv = mstat[s, pl.ds(c, 1), :]
                p = pbuf[s, c].astype(jnp.float32) * wv
                for i in range(nrow // 128):
                    total = total + p[:, i * 128 : (i + 1) * 128]
                return total

            total = lax.fori_loop(0, n, add, jnp.zeros((CH, 128), jnp.float32))
            pieces.append(jnp.sum(total.T, axis=0, keepdims=True))
        isend[j] = jnp.broadcast_to(jnp.concatenate(pieces, axis=1), isend.shape[1:])

    for d in range(1, kvh):
        i_copy(d).start()
    for d in range(1, kvh):
        s = lax.rem(head + d, kvh)
        arrived(isend.at[s], ibuf.at[s], i_s.at[d], i_r.at[s])
    ibuf[head] = isend[head]
    factor = rows * n / (kvh * group * tq * n)
    imp_ref[...] = jnp.sum(ibuf[...], axis=0)[0:1, :] * factor

    own_v.wait()

    @pl.loop(1, n)
    def _(d):
        s = lax.rem(me + d, n)
        arrived(picked.at[s], rbuf.at[s], v_s.at[d], v_r.at[s])

    column = jnp.bitwise_and(lanes, cap - 1)
    pos = jnp.bitwise_and(me - start_of, n - 1) + column * n
    slot = jnp.where(pos < count_of, lax.shift_right_logical(start_of + pos, shift), keep)
    keep_id = lax.broadcasted_iota(jnp.int32, (keep, rows), 0)
    place = jnp.where(keep_id == slot, 1.0, 0.0).astype(jnp.bfloat16)
    kv_ref[...] = jnp.dot(
        place, rbuf[...].reshape(rows, proj.shape[1]), preferred_element_type=jnp.float32
    ).astype(jnp.bfloat16)

    @pl.loop(1, n)
    def _(d):
        c_copy(d).wait_send()
        q_copy(d).wait_send()
        v_copy(d).wait_send()

    for d in range(1, kvh):
        k_copy(d).wait_send()
        i_copy(d).wait_send()
    for d in range(1, planes):
        l_copy(d).wait_send()


def shards(queries, visual_keys, hidden, keep_count, keep_index, norm_gain, kv_weight, kv_bias):
    n = lax.axis_size("seq")
    kvh = visual_keys.shape[1] // HD
    rows, width = hidden.shape
    out_w = kv_weight.shape[1]
    tq = queries.shape[0]
    hw = queries.shape[1] // kvh
    nrow = hw // HD * tq
    cap = rows // n
    planes = n // kvh
    nch = kvh * rows // CH
    steps = width // KSTEP
    f32, bf16 = jnp.float32, jnp.bfloat16
    dma = pltpu.SemaphoreType.DMA
    hbm = pl.BlockSpec(memory_space=pl.ANY)
    vmem = pl.BlockSpec(memory_space=pltpu.VMEM)
    counts = jnp.broadcast_to(keep_count[:, None], (8, rows))
    importance, layer_kv = pl.pallas_call(
        functools.partial(body, n, kvh),
        out_shape=(
            jax.ShapeDtypeStruct((1, rows), f32),
            jax.ShapeDtypeStruct((rows // 2, out_w), bf16),
        ),
        in_specs=[hbm, hbm, hbm, hbm, vmem, vmem, hbm, vmem],
        out_specs=(vmem, vmem),
        scratch_shapes=[
            pltpu.VMEM((n, tq, hw), bf16),
            pltpu.VMEM((kvh, rows, HD), bf16),
            pltpu.VMEM((steps, rows, KSTEP), bf16),
            pltpu.VMEM((steps, KSTEP, out_w), bf16),
            pltpu.VMEM((n, 8, rows), jnp.int32),
            pltpu.VMEM((rows, 128), f32),
            pltpu.VMEM((rows, out_w), f32),
            pltpu.VMEM((rows, out_w), bf16),
            pltpu.VMEM((n, cap, out_w), bf16),
            pltpu.VMEM((n, cap, out_w), bf16),
            pltpu.VMEM((n, nch, CH, nrow), bf16),
            pltpu.VMEM((n, nch, nrow), f32),
            pltpu.VMEM((n, nch, nrow), f32),
            pltpu.VMEM((n, nrow), f32),
            pltpu.VMEM((planes, n, nrow), f32),
            pltpu.VMEM((kvh, 8, rows), f32),
            pltpu.VMEM((kvh, 8, rows), f32),
            dma((steps,)), dma((steps,)), dma((4,)),
            dma((n,)), dma((n,)), dma((kvh,)), dma((kvh,)),
            dma((n,)), dma((n,)), dma((n,)), dma((n,)),
            dma((planes,)), dma((planes,)), dma((kvh,)), dma((kvh,)),
        ],
        compiler_params=pltpu.CompilerParams(
            collective_id=0, has_side_effects=True, vmem_limit_bytes=66 * 1000 * 1000
        ),
    )(
        queries, visual_keys, hidden, counts, keep_index.reshape(1, rows),
        norm_gain.reshape(1, width), kv_weight, kv_bias.reshape(1, out_w),
    )
    return (importance.reshape(rows), layer_kv)


def solution(mesh):
    placed = (
        P(("groups", "seq"), None),
        P(("groups", "seq"), None),
        P(("groups", "seq"), None),
        P(("groups", "seq")),
        P(("groups", "seq")),
        P(),
        P(),
        P(),
    )
    return jax.shard_map(
        shards,
        mesh=mesh,
        in_specs=placed,
        out_specs=(P(("groups", "seq")), P(("groups", "seq"), None)),
        check_vma=False,
    )
```

```python
import functools

import jax
import jax.numpy as jnp
from jax import lax
from jax.experimental import pallas as pl
from jax.experimental.pallas import tpu as pltpu
from jax.sharding import PartitionSpec as P

HD = 128
EPS = 1e-6
CH = 128
KSTEP = 1024
MESH = pl.DeviceIdType.MESH
NT_DIMS = (((1,), (1,)), ((), ()))
LOG2E = 1.4426950408889634


def body(
    n, kvh, q_hbm, k_hbm, h_hbm, cnt_hbm, idx_ref, gain_ref, w_hbm, bias_ref,
    imp_ref, kv_ref,
    qbuf, kbuf, hid, wbuf, cnt, ssq, acc, proj, picked, rbuf, pbuf, mstat, lstat,
    lsend, lbuf, isend, ibuf, pick,
    h_sem, w_sem, loc_sem, q_s, q_r, k_s, k_r, c_s, c_r, v_s, v_r, l_s, l_r, i_s, i_r,
    up_s, down_s, block_r,
):
    me = lax.axis_index("seq")
    planes = n // kvh
    head = lax.rem(me, kvh)
    plane = me // kvh
    rows, tq = h_hbm.shape[0], q_hbm.shape[0]
    width = h_hbm.shape[1]
    steps = width // KSTEP
    hw = q_hbm.shape[1] // kvh
    group = hw // HD
    nrow = group * tq
    cap = rows // n
    shift, cap_shift = n.bit_length() - 1, cap.bit_length() - 1
    keep = kv_ref.shape[0]
    nch = kvh * rows // CH
    scale = HD**-0.5 * LOG2E

    def h_copy(k):
        return pltpu.make_async_copy(
            h_hbm.at[:, pl.ds(pl.multiple_of(k * KSTEP, KSTEP), KSTEP)], hid.at[k], h_sem.at[k]
        )

    def w_copy(k):
        return pltpu.make_async_copy(
            w_hbm.at[pl.ds(pl.multiple_of(k * KSTEP, KSTEP), KSTEP), :], wbuf.at[k], w_sem.at[k]
        )

    def remote(src, dst, ssem, rsem, peer):
        return pltpu.make_async_remote_copy(
            src_ref=src, dst_ref=dst, send_sem=ssem, recv_sem=rsem,
            device_id={"seq": peer}, device_id_type=MESH,
        )

    def q_src(t):
        return q_hbm.at[:, pl.ds(pl.multiple_of(t * hw, hw), hw)]

    def k_src(t):
        return k_hbm.at[:, pl.ds(pl.multiple_of(t * HD, HD), HD)]

    for k in range(steps):
        h_copy(k).start()
    for k in range(steps):
        w_copy(k).start()
    own = [
        pltpu.make_async_copy(q_src(head), qbuf.at[plane, head], loc_sem.at[0]),
        pltpu.make_async_copy(k_src(head), kbuf.at[head], loc_sem.at[1]),
        pltpu.make_async_copy(cnt_hbm, cnt.at[me], loc_sem.at[2]),
    ]
    for c in own:
        c.start()

    bar = pltpu.get_barrier_semaphore()

    @pl.loop(1, n)
    def _(d):
        pl.semaphore_signal(bar, inc=1, device_id={"seq": lax.rem(me + d, n)}, device_id_type=MESH)

    pl.semaphore_wait(bar, n - 1)

    def c_copy(d):
        t = lax.rem(me + d, n)
        return remote(cnt_hbm, cnt.at[me], c_s.at[d], c_r.at[me], t)

    def q_copy(d):
        t = lax.rem(head + d, kvh)
        return remote(q_src(t), qbuf.at[plane, head], q_s.at[d], q_r.at[head], plane * kvh + t)

    def up_copy(t):
        p = plane - t
        return remote(qbuf.at[p], qbuf.at[p], up_s.at[t], block_r.at[p], me + kvh)

    def down_copy(t):
        p = plane + t
        return remote(qbuf.at[p], qbuf.at[p], down_s.at[t], block_r.at[p], me - kvh)

    def relays(t, act):
        @pl.when(jnp.logical_and(plane - t >= 0, plane + 1 < planes))
        def _():
            act(up_copy(t))

        @pl.when(jnp.logical_and(plane + t < planes, plane >= 1))
        def _():
            act(down_copy(t))

    def send_on(t):
        relays(t, lambda c: c.start())

    def receive(t):
        @pl.when(plane - t >= 0)
        def _():
            arrived(qbuf.at[plane - t], qbuf.at[plane - t], up_s.at[t], block_r.at[plane - t])

        @pl.when(plane + t < planes)
        def _():
            arrived(qbuf.at[plane + t], qbuf.at[plane + t], down_s.at[t], block_r.at[plane + t])

    def k_copy(d):
        t = lax.rem(head + d, kvh)
        return remote(k_src(t), kbuf.at[head], k_s.at[d], k_r.at[head], plane * kvh + t)

    def v_copy(d):
        t = lax.rem(me + d, n)
        return remote(picked.at[t], rbuf.at[me], v_s.at[d], v_r.at[me], t)

    def l_copy(d):
        t = lax.rem(plane + d, planes)
        return remote(lsend, lbuf.at[plane], l_s.at[d], l_r.at[plane], t * kvh + head)

    def i_copy(d):
        t = lax.rem(head + d, kvh)
        return remote(isend.at[t], ibuf.at[head], i_s.at[d], i_r.at[head], plane * kvh + t)

    def arrived(src, dst, ssem, rsem):
        remote(src, dst, ssem, rsem, lax.rem(me + 1, n)).wait_recv()

    @pl.loop(1, n)
    def _(d):
        c_copy(d).start()

    for d in range(1, kvh):
        q_copy(d).start()
    for d in range(1, kvh):
        k_copy(d).start()

    ssq[...] = jnp.zeros_like(ssq)

    @pl.loop(0, steps)
    def _(k):
        h_copy(k).wait()
        x = hid[k].astype(jnp.float32)
        x = x * x
        part = x[:, :128]
        for j in range(1, KSTEP // 128):
            part += x[:, j * 128 : (j + 1) * 128]
        ssq[...] += part

    inv = lax.rsqrt(jnp.sum(ssq[...], axis=1, keepdims=True) / width + EPS)
    ssq[...] = jnp.broadcast_to(inv, ssq.shape)
    acc[...] = jnp.broadcast_to(bias_ref[...], acc.shape)

    own[0].wait()
    for d in range(1, kvh):
        s = lax.rem(head + d, kvh)
        arrived(q_src(s), qbuf.at[plane, s], q_s.at[d], q_r.at[s])
    send_on(0)

    own[2].wait()

    @pl.loop(1, n)
    def _(d):
        s = lax.rem(me + d, n)
        arrived(cnt_hbm, cnt.at[s], c_s.at[d], c_r.at[s])

    lanes = lax.broadcasted_iota(jnp.int32, (1, rows), 1)
    source = lax.shift_right_logical(lanes, cap_shift)
    run = jnp.zeros((1, rows), jnp.int32)
    start_of = jnp.zeros((1, rows), jnp.int32)
    count_of = jnp.zeros((1, rows), jnp.int32)
    my_start = jnp.zeros((1, rows), jnp.int32)
    for s in range(n):
        c = cnt[s, 0:1, :]
        start_of = jnp.where(source == s, run, start_of)
        count_of = jnp.where(source == s, c, count_of)
        my_start = my_start + jnp.where(s < me, c, 0)
        run = run + c

    row_id = lax.broadcasted_iota(jnp.int32, (rows, rows), 0)
    lane_id = lax.broadcasted_iota(jnp.int32, (rows, rows), 1)
    is_row = jnp.where(row_id == idx_ref[...], 1.0, 0.0).astype(jnp.bfloat16)
    owner = lax.shift_right_logical(row_id, cap_shift)
    column = jnp.bitwise_and(row_id, cap - 1)
    pos = jnp.bitwise_and(owner - my_start, n - 1) + column * n
    is_pos = jnp.where(pos == lane_id, 1.0, 0.0).astype(jnp.bfloat16)
    pick[...] = lax.dot_general(
        is_pos, is_row, NT_DIMS, preferred_element_type=jnp.float32
    ).astype(jnp.bfloat16)


    @pl.loop(0, steps)
    def _(k):
        w_copy(k).wait()
        g = gain_ref[:, pl.ds(pl.multiple_of(k * KSTEP, KSTEP), KSTEP)]
        normed = (hid[k].astype(jnp.float32) * ssq[:, 0:1] * g).astype(jnp.bfloat16)
        acc[...] += jnp.dot(normed, wbuf[k], preferred_element_type=jnp.float32)

    proj[...] = acc[...].astype(jnp.bfloat16)
    if planes > 1:
        receive(1)
        send_on(1)

    out = jnp.dot(pick[...], proj[...], preferred_element_type=jnp.float32).astype(jnp.bfloat16)
    picked[...] = out.reshape(picked.shape)

    @pl.loop(n // 2, n)
    def _(d):
        v_copy(d).start()

    own_v = pltpu.make_async_copy(picked.at[me], rbuf.at[me], loc_sem.at[3])
    own_v.start()

    own[1].wait()
    for d in range(1, kvh):
        s = lax.rem(head + d, kvh)
        arrived(k_src(s), kbuf.at[s], k_s.at[d], k_r.at[s])

    def score(s):
        q = jnp.concatenate([qbuf[s // kvh, s % kvh, :, g * HD : (g + 1) * HD] for g in range(group)], axis=0)
        for c in range(nch):
            j, part = divmod(c * CH, rows)
            keys = kbuf[j, part : part + CH, :]
            t = lax.dot_general(keys, q, NT_DIMS, preferred_element_type=jnp.float32)
            top = jnp.max(t, axis=0, keepdims=True)
            p = jnp.exp2((t - top) * scale)
            mstat[s, c : c + 1, :] = top * scale
            lstat[s, c : c + 1, :] = jnp.sum(p, axis=0, keepdims=True)
            pbuf[s, c] = p.astype(jnp.bfloat16)

    @pl.loop(0, 2 * planes - 1)
    def _(u):
        t = (u + 1) // 2
        below = lax.rem(u, 2) == 1
        p = jnp.where(below, plane - t, plane + t)

        @pl.when(jnp.logical_and(below, t > 1))
        def _():
            receive(t)
            send_on(t)

        @pl.when(jnp.logical_and(p >= 0, p < planes))
        def _():
            @pl.loop(0, kvh)
            def _(i):
                score(p * kvh + i)

    for s in range(n):
        m = mstat[s]
        top = jnp.max(m, axis=0, keepdims=True)
        total = jnp.sum(lstat[s] * jnp.exp2(m - top), axis=0, keepdims=True)
        lsend[s : s + 1, :] = top + jnp.log2(total)
    for d in range(1, planes):
        l_copy(d).start()

    @pl.loop(1, n // 2)
    def _(d):
        v_copy(d).start()

    for d in range(1, planes):
        s = lax.rem(plane + d, planes)
        arrived(lsend, lbuf.at[s], l_s.at[d], l_r.at[s])
    lbuf[plane] = lsend[...]
    lse = lbuf[...]
    top = jnp.max(lse, axis=0)
    lse = top + jnp.log2(jnp.sum(jnp.exp2(lse - top[None]), axis=0))
    for s in range(n):
        mstat[s] = jnp.exp2(mstat[s] - lse[s : s + 1, :])

    @pl.loop(0, kvh)
    def _(j):
        pieces = []
        for part in range(rows // CH):
            c = j * (rows // CH) + part

            def add(s, total):
                wv = mstat[s, pl.ds(c, 1), :]
                p = pbuf[s, c].astype(jnp.float32) * wv
                for i in range(nrow // 128):
                    total = total + p[:, i * 128 : (i + 1) * 128]
                return total

            total = lax.fori_loop(0, n, add, jnp.zeros((CH, 128), jnp.float32), unroll=8)
            pieces.append(jnp.sum(total.T, axis=0, keepdims=True))
        isend[j] = jnp.broadcast_to(jnp.concatenate(pieces, axis=1), isend.shape[1:])

    for d in range(1, kvh):
        i_copy(d).start()
    for d in range(1, kvh):
        s = lax.rem(head + d, kvh)
        arrived(isend.at[s], ibuf.at[s], i_s.at[d], i_r.at[s])
    ibuf[head] = isend[head]
    factor = rows * n / (kvh * group * tq * n)
    imp_ref[...] = jnp.sum(ibuf[...], axis=0)[0:1, :] * factor

    column = jnp.bitwise_and(lanes, cap - 1)
    pos = jnp.bitwise_and(me - start_of, n - 1) + column * n
    slot = jnp.where(pos < count_of, lax.shift_right_logical(start_of + pos, shift), keep)
    keep_id = lax.broadcasted_iota(jnp.int32, (keep, rows), 0)
    place = jnp.where(keep_id == slot, 1.0, 0.0).astype(jnp.bfloat16)
    own_v.wait()

    @pl.loop(1, n)
    def _(d):
        s = lax.rem(me + d, n)
        arrived(picked.at[s], rbuf.at[s], v_s.at[d], v_r.at[s])

    kv_ref[...] = jnp.dot(
        place, rbuf[...].reshape(rows, proj.shape[1]), preferred_element_type=jnp.float32
    ).astype(jnp.bfloat16)

    @pl.loop(1, n)
    def _(d):
        c_copy(d).wait_send()
        v_copy(d).wait_send()

    for d in range(1, kvh):
        q_copy(d).wait_send()
        k_copy(d).wait_send()
        i_copy(d).wait_send()
    for d in range(1, planes):
        l_copy(d).wait_send()

    @pl.loop(0, planes)
    def _(t):
        relays(t, lambda c: c.wait_send())


def shards(queries, visual_keys, hidden, keep_count, keep_index, norm_gain, kv_weight, kv_bias):
    n = lax.axis_size("seq")
    kvh = visual_keys.shape[1] // HD
    rows, width = hidden.shape
    out_w = kv_weight.shape[1]
    tq = queries.shape[0]
    hw = queries.shape[1] // kvh
    nrow = hw // HD * tq
    cap = rows // n
    planes = n // kvh
    nch = kvh * rows // CH
    steps = width // KSTEP
    f32, bf16 = jnp.float32, jnp.bfloat16
    dma = pltpu.SemaphoreType.DMA
    hbm = pl.BlockSpec(memory_space=pl.ANY)
    vmem = pl.BlockSpec(memory_space=pltpu.VMEM)
    counts = jnp.broadcast_to(keep_count[:, None], (8, rows))
    importance, layer_kv = pl.pallas_call(
        functools.partial(body, n, kvh),
        out_shape=(
            jax.ShapeDtypeStruct((1, rows), f32),
            jax.ShapeDtypeStruct((rows // 2, out_w), bf16),
        ),
        in_specs=[hbm, hbm, hbm, hbm, vmem, vmem, hbm, vmem],
        out_specs=(vmem, vmem),
        scratch_shapes=[
            pltpu.VMEM((planes, kvh, tq, hw), bf16),
            pltpu.VMEM((kvh, rows, HD), bf16),
            pltpu.VMEM((steps, rows, KSTEP), bf16),
            pltpu.VMEM((steps, KSTEP, out_w), bf16),
            pltpu.VMEM((n, 8, rows), jnp.int32),
            pltpu.VMEM((rows, 128), f32),
            pltpu.VMEM((rows, out_w), f32),
            pltpu.VMEM((rows, out_w), bf16),
            pltpu.VMEM((n, cap, out_w), bf16),
            pltpu.VMEM((n, cap, out_w), bf16),
            pltpu.VMEM((n, nch, CH, nrow), bf16),
            pltpu.VMEM((n, nch, nrow), f32),
            pltpu.VMEM((n, nch, nrow), f32),
            pltpu.VMEM((n, nrow), f32),
            pltpu.VMEM((planes, n, nrow), f32),
            pltpu.VMEM((kvh, 8, rows), f32),
            pltpu.VMEM((kvh, 8, rows), f32),
            pltpu.VMEM((rows, rows), bf16),
            dma((steps,)), dma((steps,)), dma((4,)),
            dma((kvh,)), dma((kvh,)), dma((kvh,)), dma((kvh,)),
            dma((n,)), dma((n,)), dma((n,)), dma((n,)),
            dma((planes,)), dma((planes,)), dma((kvh,)), dma((kvh,)),
            dma((planes,)), dma((planes,)), dma((planes,)),
        ],
        compiler_params=pltpu.CompilerParams(
            collective_id=0, has_side_effects=True, vmem_limit_bytes=66 * 1000 * 1000
        ),
    )(
        queries, visual_keys, hidden, counts, keep_index.reshape(1, rows),
        norm_gain.reshape(1, width), kv_weight, kv_bias.reshape(1, out_w),
    )
    return (importance.reshape(rows), layer_kv)


def solution(mesh):
    placed = (
        P(("groups", "seq"), None),
        P(("groups", "seq"), None),
        P(("groups", "seq"), None),
        P(("groups", "seq")),
        P(("groups", "seq")),
        P(),
        P(),
        P(),
    )
    return jax.shard_map(
        shards,
        mesh=mesh,
        in_specs=placed,
        out_specs=(P(("groups", "seq")), P(("groups", "seq"), None)),
        check_vma=False,
    )
```

```python
import functools

import jax
import jax.numpy as jnp
from jax import lax
from jax.experimental import pallas as pl
from jax.experimental.pallas import tpu as pltpu
from jax.sharding import PartitionSpec as P

HD = 128
EPS = 1e-6
CH = 128
KSTEP = 1024
MESH = pl.DeviceIdType.MESH
NT_DIMS = (((1,), (1,)), ((), ()))
LOG2E = 1.4426950408889634


def body(
    n, kvh, q_hbm, k_hbm, h_hbm, cnt_hbm, idx_ref, gain_ref, w_hbm, bias_ref,
    imp_ref, kv_ref,
    qbuf, kbuf, hid, wbuf, cnt, ssq, acc, proj, picked, rbuf, pbuf, mstat, lstat,
    lsend, lbuf, isend, ibuf, pick,
    h_sem, w_sem, loc_sem, q_s, q_r, k_s, k_r, c_s, c_r, v_s, v_r, l_s, l_r, i_s, i_r,
    up_s, down_s, block_r,
):
    me = lax.axis_index("seq")
    planes = n // kvh
    head = lax.rem(me, kvh)
    plane = me // kvh
    rows, tq = h_hbm.shape[0], q_hbm.shape[0]
    width = h_hbm.shape[1]
    steps = width // KSTEP
    hw = q_hbm.shape[1] // kvh
    group = hw // HD
    nrow = group * tq
    cap = rows // n
    shift, cap_shift = n.bit_length() - 1, cap.bit_length() - 1
    keep = kv_ref.shape[0]
    nch = kvh * rows // CH
    scale = HD**-0.5 * LOG2E

    def h_copy(k):
        return pltpu.make_async_copy(
            h_hbm.at[:, pl.ds(pl.multiple_of(k * KSTEP, KSTEP), KSTEP)], hid.at[k], h_sem.at[k]
        )

    def w_copy(k):
        return pltpu.make_async_copy(
            w_hbm.at[pl.ds(pl.multiple_of(k * KSTEP, KSTEP), KSTEP), :], wbuf.at[k], w_sem.at[k]
        )

    def remote(src, dst, ssem, rsem, peer):
        return pltpu.make_async_remote_copy(
            src_ref=src, dst_ref=dst, send_sem=ssem, recv_sem=rsem,
            device_id={"seq": peer}, device_id_type=MESH,
        )

    def q_src(t):
        return q_hbm.at[:, pl.ds(pl.multiple_of(t * hw, hw), hw)]

    def k_src(t):
        return k_hbm.at[:, pl.ds(pl.multiple_of(t * HD, HD), HD)]

    for k in range(steps):
        h_copy(k).start()
    for k in range(steps):
        w_copy(k).start()
    own = [
        pltpu.make_async_copy(q_src(head), qbuf.at[plane, head], loc_sem.at[0]),
        pltpu.make_async_copy(k_src(head), kbuf.at[head], loc_sem.at[1]),
        pltpu.make_async_copy(cnt_hbm, cnt.at[me], loc_sem.at[2]),
    ]
    for c in own:
        c.start()

    bar = pltpu.get_barrier_semaphore()

    @pl.loop(1, n)
    def _(d):
        pl.semaphore_signal(bar, inc=1, device_id={"seq": lax.rem(me + d, n)}, device_id_type=MESH)

    pl.semaphore_wait(bar, n - 1)

    def c_copy(d):
        t = lax.rem(me + d, n)
        return remote(cnt_hbm, cnt.at[me], c_s.at[d], c_r.at[me], t)

    def q_copy(d):
        t = lax.rem(head + d, kvh)
        return remote(q_src(t), qbuf.at[plane, head], q_s.at[d], q_r.at[head], plane * kvh + t)

    def up_copy(t):
        p = plane - t
        return remote(qbuf.at[p], qbuf.at[p], up_s.at[t], block_r.at[p], me + kvh)

    def down_copy(t):
        p = plane + t
        return remote(qbuf.at[p], qbuf.at[p], down_s.at[t], block_r.at[p], me - kvh)

    def relays(t, act):
        @pl.when(jnp.logical_and(plane - t >= 0, plane + 1 < planes))
        def _():
            act(up_copy(t))

        @pl.when(jnp.logical_and(plane + t < planes, plane >= 1))
        def _():
            act(down_copy(t))

    def send_on(t):
        relays(t, lambda c: c.start())

    def receive(t):
        @pl.when(plane - t >= 0)
        def _():
            arrived(qbuf.at[plane - t], qbuf.at[plane - t], up_s.at[t], block_r.at[plane - t])

        @pl.when(plane + t < planes)
        def _():
            arrived(qbuf.at[plane + t], qbuf.at[plane + t], down_s.at[t], block_r.at[plane + t])

    def k_copy(d):
        t = lax.rem(head + d, kvh)
        return remote(k_src(t), kbuf.at[head], k_s.at[d], k_r.at[head], plane * kvh + t)

    def v_copy(d):
        t = lax.rem(me + d, n)
        return remote(picked.at[t], rbuf.at[me], v_s.at[d], v_r.at[me], t)

    def l_copy(d):
        t = lax.rem(plane + d, planes)
        return remote(lsend, lbuf.at[plane], l_s.at[d], l_r.at[plane], t * kvh + head)

    def i_copy(d):
        t = lax.rem(head + d, kvh)
        return remote(isend.at[t], ibuf.at[head], i_s.at[d], i_r.at[head], plane * kvh + t)

    def arrived(src, dst, ssem, rsem):
        remote(src, dst, ssem, rsem, lax.rem(me + 1, n)).wait_recv()

    for d in range(1, kvh):
        q_copy(d).start()

    @pl.loop(1, n)
    def _(d):
        c_copy(d).start()

    for d in range(1, kvh):
        k_copy(d).start()

    ssq[...] = jnp.zeros_like(ssq)

    @pl.loop(0, steps)
    def _(k):
        h_copy(k).wait()
        x = hid[k].astype(jnp.float32)
        x = x * x
        part = x[:, :128]
        for j in range(1, KSTEP // 128):
            part += x[:, j * 128 : (j + 1) * 128]
        ssq[...] += part

    inv = lax.rsqrt(jnp.sum(ssq[...], axis=1, keepdims=True) / width + EPS)
    ssq[...] = jnp.broadcast_to(inv, ssq.shape)
    acc[...] = jnp.broadcast_to(bias_ref[...], acc.shape)

    own[0].wait()
    for d in range(1, kvh):
        s = lax.rem(head + d, kvh)
        arrived(q_src(s), qbuf.at[plane, s], q_s.at[d], q_r.at[s])
    send_on(0)

    own[2].wait()

    @pl.loop(1, n)
    def _(d):
        s = lax.rem(me + d, n)
        arrived(cnt_hbm, cnt.at[s], c_s.at[d], c_r.at[s])

    lanes = lax.broadcasted_iota(jnp.int32, (1, rows), 1)
    source = lax.shift_right_logical(lanes, cap_shift)
    run = jnp.zeros((1, rows), jnp.int32)
    start_of = jnp.zeros((1, rows), jnp.int32)
    count_of = jnp.zeros((1, rows), jnp.int32)
    my_start = jnp.zeros((1, rows), jnp.int32)
    for s in range(n):
        c = jnp.concatenate([cnt[s]] * (rows // 128), axis=1)
        start_of = jnp.where(source == s, run, start_of)
        count_of = jnp.where(source == s, c, count_of)
        my_start = my_start + jnp.where(s < me, c, 0)
        run = run + c

    row_id = lax.broadcasted_iota(jnp.int32, (rows, rows), 0)
    lane_id = lax.broadcasted_iota(jnp.int32, (rows, rows), 1)
    is_row = jnp.where(row_id == idx_ref[...], 1.0, 0.0).astype(jnp.bfloat16)
    owner = lax.shift_right_logical(row_id, cap_shift)
    column = jnp.bitwise_and(row_id, cap - 1)
    pos = jnp.bitwise_and(owner - my_start, n - 1) + column * n
    is_pos = jnp.where(pos == lane_id, 1.0, 0.0).astype(jnp.bfloat16)
    pick[...] = lax.dot_general(
        is_pos, is_row, NT_DIMS, preferred_element_type=jnp.float32
    ).astype(jnp.bfloat16)


    @pl.loop(0, steps)
    def _(k):
        w_copy(k).wait()
        g = gain_ref[:, pl.ds(pl.multiple_of(k * KSTEP, KSTEP), KSTEP)]
        normed = (hid[k].astype(jnp.float32) * ssq[:, 0:1] * g).astype(jnp.bfloat16)
        acc[...] += jnp.dot(normed, wbuf[k], preferred_element_type=jnp.float32)

        @pl.when(k == steps - 2)
        def _():
            receive(1)
            send_on(1)

    proj[...] = acc[...].astype(jnp.bfloat16)

    out = jnp.dot(pick[...], proj[...], preferred_element_type=jnp.float32).astype(jnp.bfloat16)
    picked[...] = out.reshape(picked.shape)

    def send_rows(first, last):
        @pl.loop(first, last)
        def _(d):
            v_copy(d).start()

    send_rows(n // 2, 3 * n // 4)

    own_v = pltpu.make_async_copy(picked.at[me], rbuf.at[me], loc_sem.at[3])
    own_v.start()

    own[1].wait()
    for d in range(1, kvh):
        s = lax.rem(head + d, kvh)
        arrived(k_src(s), kbuf.at[s], k_s.at[d], k_r.at[s])

    def score(s):
        q = jnp.concatenate([qbuf[s // kvh, s % kvh, :, g * HD : (g + 1) * HD] for g in range(group)], axis=0)
        for c in range(nch):
            j, part = divmod(c * CH, rows)
            keys = kbuf[j, part : part + CH, :]
            t = lax.dot_general(keys, q, NT_DIMS, preferred_element_type=jnp.float32)
            top = jnp.max(t, axis=0, keepdims=True)
            p = jnp.exp2((t - top) * scale)
            mstat[s, c : c + 1, :] = top * scale
            lstat[s, c : c + 1, :] = jnp.sum(p, axis=0, keepdims=True)
            pbuf[s, c] = p.astype(jnp.bfloat16)

    @pl.loop(0, 2 * planes - 1)
    def _(u):
        t = (u + 1) // 2
        below = lax.rem(u, 2) == 1
        p = jnp.where(below, plane - t, plane + t)

        @pl.when(jnp.logical_and(below, t > 1))
        def _():
            receive(t)
            send_on(t)

            @pl.when(t == 2)
            def _():
                send_rows(3 * n // 4, n)

            @pl.when(t == planes - 1)
            def _():
                send_rows(n // 4, n // 2)

        @pl.when(jnp.logical_and(p >= 0, p < planes))
        def _():
            @pl.loop(0, kvh)
            def _(i):
                score(p * kvh + i)

    for s in range(n):
        m = mstat[s]
        top = jnp.max(m, axis=0, keepdims=True)
        total = jnp.sum(lstat[s] * jnp.exp2(m - top), axis=0, keepdims=True)
        lsend[s : s + 1, :] = top + jnp.log2(total)
    for d in range(1, planes):
        l_copy(d).start()

    send_rows(1, n // 4)

    for d in range(1, planes):
        s = lax.rem(plane + d, planes)
        arrived(lsend, lbuf.at[s], l_s.at[d], l_r.at[s])
    lbuf[plane] = lsend[...]
    lse = lbuf[...]
    top = jnp.max(lse, axis=0)
    lse = top + jnp.log2(jnp.sum(jnp.exp2(lse - top[None]), axis=0))
    for s in range(n):
        mstat[s] = jnp.exp2(mstat[s] - lse[s : s + 1, :])

    @pl.loop(0, kvh)
    def _(j):
        pieces = []
        for part in range(rows // CH):
            c = j * (rows // CH) + part

            def add(s, total):
                wv = mstat[s, pl.ds(c, 1), :]
                p = pbuf[s, c].astype(jnp.float32) * wv
                for i in range(nrow // 128):
                    total = total + p[:, i * 128 : (i + 1) * 128]
                return total

            total = lax.fori_loop(0, n, add, jnp.zeros((CH, 128), jnp.float32), unroll=8)
            pieces.append(jnp.sum(total.T, axis=0, keepdims=True))
        isend[j] = jnp.broadcast_to(jnp.concatenate(pieces, axis=1), isend.shape[1:])

    for d in range(1, kvh):
        i_copy(d).start()
    for d in range(1, kvh):
        s = lax.rem(head + d, kvh)
        arrived(isend.at[s], ibuf.at[s], i_s.at[d], i_r.at[s])
    ibuf[head] = isend[head]
    factor = rows * n / (kvh * group * tq * n)
    imp_ref[...] = jnp.sum(ibuf[...], axis=0)[0:1, :] * factor

    column = jnp.bitwise_and(lanes, cap - 1)
    pos = jnp.bitwise_and(me - start_of, n - 1) + column * n
    slot = jnp.where(pos < count_of, lax.shift_right_logical(start_of + pos, shift), keep)
    keep_id = lax.broadcasted_iota(jnp.int32, (keep, rows), 0)
    place = jnp.where(keep_id == slot, 1.0, 0.0).astype(jnp.bfloat16)
    own_v.wait()

    @pl.loop(1, n)
    def _(d):
        s = lax.rem(me + d, n)
        arrived(picked.at[s], rbuf.at[s], v_s.at[d], v_r.at[s])

    kv_ref[...] = jnp.dot(
        place, rbuf[...].reshape(rows, proj.shape[1]), preferred_element_type=jnp.float32
    ).astype(jnp.bfloat16)

    @pl.loop(1, n)
    def _(d):
        c_copy(d).wait_send()
        v_copy(d).wait_send()

    for d in range(1, kvh):
        q_copy(d).wait_send()
        k_copy(d).wait_send()
        i_copy(d).wait_send()
    for d in range(1, planes):
        l_copy(d).wait_send()

    @pl.loop(0, planes)
    def _(t):
        relays(t, lambda c: c.wait_send())


def shards(queries, visual_keys, hidden, keep_count, keep_index, norm_gain, kv_weight, kv_bias):
    n = lax.axis_size("seq")
    kvh = visual_keys.shape[1] // HD
    rows, width = hidden.shape
    out_w = kv_weight.shape[1]
    tq = queries.shape[0]
    hw = queries.shape[1] // kvh
    nrow = hw // HD * tq
    cap = rows // n
    planes = n // kvh
    nch = kvh * rows // CH
    steps = width // KSTEP
    f32, bf16 = jnp.float32, jnp.bfloat16
    dma = pltpu.SemaphoreType.DMA
    hbm = pl.BlockSpec(memory_space=pl.ANY)
    vmem = pl.BlockSpec(memory_space=pltpu.VMEM)
    counts = jnp.broadcast_to(keep_count[:, None], (1, 128))
    importance, layer_kv = pl.pallas_call(
        functools.partial(body, n, kvh),
        out_shape=(
            jax.ShapeDtypeStruct((1, rows), f32),
            jax.ShapeDtypeStruct((rows // 2, out_w), bf16),
        ),
        in_specs=[hbm, hbm, hbm, hbm, vmem, vmem, hbm, vmem],
        out_specs=(vmem, vmem),
        scratch_shapes=[
            pltpu.VMEM((planes, kvh, tq, hw), bf16),
            pltpu.VMEM((kvh, rows, HD), bf16),
            pltpu.VMEM((steps, rows, KSTEP), bf16),
            pltpu.VMEM((steps, KSTEP, out_w), bf16),
            pltpu.VMEM((n, 1, 128), jnp.int32),
            pltpu.VMEM((rows, 128), f32),
            pltpu.VMEM((rows, out_w), f32),
            pltpu.VMEM((rows, out_w), bf16),
            pltpu.VMEM((n, cap, out_w), bf16),
            pltpu.VMEM((n, cap, out_w), bf16),
            pltpu.VMEM((n, nch, CH, nrow), bf16),
            pltpu.VMEM((n, nch, nrow), f32),
            pltpu.VMEM((n, nch, nrow), f32),
            pltpu.VMEM((n, nrow), f32),
            pltpu.VMEM((planes, n, nrow), f32),
            pltpu.VMEM((kvh, 8, rows), f32),
            pltpu.VMEM((kvh, 8, rows), f32),
            pltpu.VMEM((rows, rows), bf16),
            dma((steps,)), dma((steps,)), dma((4,)),
            dma((kvh,)), dma((kvh,)), dma((kvh,)), dma((kvh,)),
            dma((n,)), dma((n,)), dma((n,)), dma((n,)),
            dma((planes,)), dma((planes,)), dma((kvh,)), dma((kvh,)),
            dma((planes,)), dma((planes,)), dma((planes,)),
        ],
        compiler_params=pltpu.CompilerParams(
            collective_id=0, has_side_effects=True, vmem_limit_bytes=66 * 1000 * 1000
        ),
    )(
        queries, visual_keys, hidden, counts, keep_index.reshape(1, rows),
        norm_gain.reshape(1, width), kv_weight, kv_bias.reshape(1, out_w),
    )
    return (importance.reshape(rows), layer_kv)


def solution(mesh):
    placed = (
        P(("groups", "seq"), None),
        P(("groups", "seq"), None),
        P(("groups", "seq"), None),
        P(("groups", "seq")),
        P(("groups", "seq")),
        P(),
        P(),
        P(),
    )
    return jax.shard_map(
        shards,
        mesh=mesh,
        in_specs=placed,
        out_specs=(P(("groups", "seq")), P(("groups", "seq"), None)),
        check_vma=False,
    )
```

```python
import functools

import jax
import jax.numpy as jnp
from jax import lax
from jax.experimental import pallas as pl
from jax.experimental.pallas import tpu as pltpu
from jax.sharding import PartitionSpec as P

HD = 128
EPS = 1e-6
CH = 128
KSTEP = 1024
MESH = pl.DeviceIdType.MESH
NT_DIMS = (((1,), (1,)), ((), ()))
LOG2E = 1.4426950408889634


def body(
    n, kvh, q_hbm, k_hbm, h_hbm, cnt_hbm, idx_ref, gain_ref, w_hbm, bias_ref,
    imp_ref, kv_ref,
    qbuf, kbuf, hid, wbuf, cnt, ssq, acc, proj, picked, rbuf, pbuf, mstat, lstat,
    lsend, lbuf, isend, ibuf, pick,
    h_sem, w_sem, loc_sem, q_s, q_r, k_s, k_r, c_s, c_r, v_s, v_r, l_s, l_r, i_s, i_r,
    up_s, down_s, block_r,
):
    me = lax.axis_index("seq")
    planes = n // kvh
    head = lax.rem(me, kvh)
    plane = me // kvh
    rows, tq = h_hbm.shape[0], q_hbm.shape[0]
    width = h_hbm.shape[1]
    steps = width // KSTEP
    hw = q_hbm.shape[1] // kvh
    group = hw // HD
    nrow = group * tq
    cap = rows // n
    shift, cap_shift = n.bit_length() - 1, cap.bit_length() - 1
    keep = kv_ref.shape[0]
    nch = kvh * rows // CH
    scale = HD**-0.5 * LOG2E

    def h_copy(k):
        return pltpu.make_async_copy(
            h_hbm.at[:, pl.ds(pl.multiple_of(k * KSTEP, KSTEP), KSTEP)], hid.at[k], h_sem.at[k]
        )

    def w_copy(k):
        return pltpu.make_async_copy(
            w_hbm.at[pl.ds(pl.multiple_of(k * KSTEP, KSTEP), KSTEP), :], wbuf.at[k], w_sem.at[k]
        )

    def remote(src, dst, ssem, rsem, peer):
        return pltpu.make_async_remote_copy(
            src_ref=src, dst_ref=dst, send_sem=ssem, recv_sem=rsem,
            device_id={"seq": peer}, device_id_type=MESH,
        )

    def q_src(t):
        return q_hbm.at[:, pl.ds(pl.multiple_of(t * hw, hw), hw)]

    def k_src(t):
        return k_hbm.at[:, pl.ds(pl.multiple_of(t * HD, HD), HD)]

    for k in range(steps):
        h_copy(k).start()
    for k in range(steps):
        w_copy(k).start()
    own = [
        pltpu.make_async_copy(q_src(head), qbuf.at[plane, head], loc_sem.at[0]),
        pltpu.make_async_copy(k_src(head), kbuf.at[head], loc_sem.at[1]),
        pltpu.make_async_copy(cnt_hbm, cnt.at[me], loc_sem.at[2]),
    ]
    for c in own:
        c.start()

    bar = pltpu.get_barrier_semaphore()

    @pl.loop(1, n)
    def _(d):
        pl.semaphore_signal(bar, inc=1, device_id={"seq": lax.rem(me + d, n)}, device_id_type=MESH)

    pl.semaphore_wait(bar, n - 1)

    def c_copy(d):
        t = lax.rem(me + d, n)
        return remote(cnt_hbm, cnt.at[me], c_s.at[d], c_r.at[me], t)

    def q_copy(d):
        t = lax.rem(head + d, kvh)
        return remote(q_src(t), qbuf.at[plane, head], q_s.at[d], q_r.at[head], plane * kvh + t)

    def up_copy(t):
        p = plane - t
        return remote(qbuf.at[p], qbuf.at[p], up_s.at[t], block_r.at[p], me + kvh)

    def down_copy(t):
        p = plane + t
        return remote(qbuf.at[p], qbuf.at[p], down_s.at[t], block_r.at[p], me - kvh)

    def relays(t, act):
        @pl.when(jnp.logical_and(plane - t >= 0, plane + 1 < planes))
        def _():
            act(up_copy(t))

        @pl.when(jnp.logical_and(plane + t < planes, plane >= 1))
        def _():
            act(down_copy(t))

    def send_on(t):
        relays(t, lambda c: c.start())

    def receive(t):
        @pl.when(plane - t >= 0)
        def _():
            arrived(qbuf.at[plane - t], qbuf.at[plane - t], up_s.at[t], block_r.at[plane - t])

        @pl.when(plane + t < planes)
        def _():
            arrived(qbuf.at[plane + t], qbuf.at[plane + t], down_s.at[t], block_r.at[plane + t])

    def k_copy(d):
        t = lax.rem(head + d, kvh)
        return remote(k_src(t), kbuf.at[head], k_s.at[d], k_r.at[head], plane * kvh + t)

    def v_copy(d):
        t = lax.rem(me + d, n)
        return remote(picked.at[t], rbuf.at[me], v_s.at[d], v_r.at[me], t)

    def l_copy(d):
        t = lax.rem(plane + d, planes)
        return remote(lsend, lbuf.at[plane], l_s.at[d], l_r.at[plane], t * kvh + head)

    def i_copy(d):
        t = lax.rem(head + d, kvh)
        return remote(isend.at[t], ibuf.at[head], i_s.at[d], i_r.at[head], plane * kvh + t)

    def arrived(src, dst, ssem, rsem):
        remote(src, dst, ssem, rsem, lax.rem(me + 1, n)).wait_recv()

    for d in range(1, kvh):
        q_copy(d).start()

    @pl.loop(1, n)
    def _(d):
        c_copy(d).start()

    for d in range(1, kvh):
        k_copy(d).start()

    ssq[...] = jnp.zeros_like(ssq)

    @pl.loop(0, steps)
    def _(k):
        h_copy(k).wait()
        x = hid[k].astype(jnp.float32)
        x = x * x
        part = x[:, :128]
        for j in range(1, KSTEP // 128):
            part += x[:, j * 128 : (j + 1) * 128]
        ssq[...] += part

    inv = lax.rsqrt(jnp.sum(ssq[...], axis=1, keepdims=True) / width + EPS)
    ssq[...] = jnp.broadcast_to(inv, ssq.shape)
    acc[...] = jnp.broadcast_to(bias_ref[...], acc.shape)

    own[0].wait()
    for d in range(1, kvh):
        s = lax.rem(head + d, kvh)
        arrived(q_src(s), qbuf.at[plane, s], q_s.at[d], q_r.at[s])
    send_on(0)

    own[2].wait()

    @pl.loop(1, n)
    def _(d):
        s = lax.rem(me + d, n)
        arrived(cnt_hbm, cnt.at[s], c_s.at[d], c_r.at[s])

    lanes = lax.broadcasted_iota(jnp.int32, (1, rows), 1)
    source = lax.shift_right_logical(lanes, cap_shift)
    run = jnp.zeros((1, rows), jnp.int32)
    start_of = jnp.zeros((1, rows), jnp.int32)
    count_of = jnp.zeros((1, rows), jnp.int32)
    my_start = jnp.zeros((1, rows), jnp.int32)
    for s in range(n):
        c = jnp.concatenate([cnt[s]] * (rows // 128), axis=1)
        start_of = jnp.where(source == s, run, start_of)
        count_of = jnp.where(source == s, c, count_of)
        my_start = my_start + jnp.where(s < me, c, 0)
        run = run + c

    row_id = lax.broadcasted_iota(jnp.int32, (rows, rows), 0)
    lane_id = lax.broadcasted_iota(jnp.int32, (rows, rows), 1)
    is_row = jnp.where(row_id == idx_ref[...], 1.0, 0.0).astype(jnp.bfloat16)
    owner = lax.shift_right_logical(row_id, cap_shift)
    column = jnp.bitwise_and(row_id, cap - 1)
    pos = jnp.bitwise_and(owner - my_start, n - 1) + column * n
    is_pos = jnp.where(pos == lane_id, 1.0, 0.0).astype(jnp.bfloat16)
    pick[...] = lax.dot_general(
        is_pos, is_row, NT_DIMS, preferred_element_type=jnp.float32
    ).astype(jnp.bfloat16)


    @pl.loop(0, steps)
    def _(k):
        w_copy(k).wait()
        g = gain_ref[:, pl.ds(pl.multiple_of(k * KSTEP, KSTEP), KSTEP)]
        normed = (hid[k].astype(jnp.float32) * ssq[:, 0:1] * g).astype(jnp.bfloat16)
        acc[...] += jnp.dot(normed, wbuf[k], preferred_element_type=jnp.float32)

        @pl.when(k == steps - 2)
        def _():
            receive(1)
            send_on(1)

    proj[...] = acc[...].astype(jnp.bfloat16)

    out = jnp.dot(pick[...], proj[...], preferred_element_type=jnp.float32).astype(jnp.bfloat16)
    picked[...] = out.reshape(picked.shape)

    def send_rows(first, last):
        @pl.loop(first, last)
        def _(d):
            v_copy(d).start()

    send_rows(n // 2, 3 * n // 4)

    own_v = pltpu.make_async_copy(picked.at[me], rbuf.at[me], loc_sem.at[3])
    own_v.start()

    own[1].wait()
    for d in range(1, kvh):
        s = lax.rem(head + d, kvh)
        arrived(k_src(s), kbuf.at[s], k_s.at[d], k_r.at[s])

    def score(s):
        q = jnp.concatenate([qbuf[s // kvh, s % kvh, :, g * HD : (g + 1) * HD] for g in range(group)], axis=0)
        for c in range(nch):
            j, part = divmod(c * CH, rows)
            keys = kbuf[j, part : part + CH, :]
            t = lax.dot_general(keys, q, NT_DIMS, preferred_element_type=jnp.float32)
            top = jnp.max(t, axis=0, keepdims=True)
            p = jnp.exp2((t - top) * scale)
            mstat[s, c : c + 1, :] = top * scale
            lstat[s, c : c + 1, :] = jnp.sum(p, axis=0, keepdims=True)
            pbuf[s, c] = p.astype(jnp.bfloat16)

    @pl.loop(0, 2 * planes - 1)
    def _(u):
        t = (u + 1) // 2
        below = lax.rem(u, 2) == 1
        p = jnp.where(below, plane - t, plane + t)

        @pl.when(jnp.logical_and(below, t > 1))
        def _():
            receive(t)
            send_on(t)

            @pl.when(t == 2)
            def _():
                send_rows(3 * n // 4, n)

            @pl.when(t == planes - 1)
            def _():
                send_rows(n // 4, n // 2)

        @pl.when(jnp.logical_and(p >= 0, p < planes))
        def _():
            @pl.loop(0, kvh)
            def _(i):
                score(p * kvh + i)

    for s in range(n):
        m = mstat[s]
        top = jnp.max(m, axis=0, keepdims=True)
        total = jnp.sum(lstat[s] * jnp.exp2(m - top), axis=0, keepdims=True)
        lsend[s : s + 1, :] = top + jnp.log2(total)
    for d in range(1, planes):
        l_copy(d).start()

    send_rows(1, n // 4)

    for d in range(1, planes):
        s = lax.rem(plane + d, planes)
        arrived(lsend, lbuf.at[s], l_s.at[d], l_r.at[s])
    lbuf[plane] = lsend[...]
    lse = lbuf[...]
    top = jnp.max(lse, axis=0)
    lse = top + jnp.log2(jnp.sum(jnp.exp2(lse - top[None]), axis=0))
    for s in range(n):
        mstat[s] = jnp.exp2(mstat[s] - lse[s : s + 1, :])

    @pl.loop(0, kvh)
    def _(j):
        pieces = []
        for part in range(rows // CH):
            c = j * (rows // CH) + part

            def add(s, total):
                wv = mstat[s, pl.ds(c, 1), :]
                p = pbuf[s, c].astype(jnp.float32) * wv
                for i in range(nrow // 128):
                    total = total + p[:, i * 128 : (i + 1) * 128]
                return total

            total = lax.fori_loop(0, n, add, jnp.zeros((CH, 128), jnp.float32), unroll=8)
            pieces.append(jnp.sum(total.T, axis=0, keepdims=True))
        isend[j] = jnp.concatenate(pieces, axis=1)

    for d in range(1, kvh):
        i_copy(d).start()
    for d in range(1, kvh):
        s = lax.rem(head + d, kvh)
        arrived(isend.at[s], ibuf.at[s], i_s.at[d], i_r.at[s])
    ibuf[head] = isend[head]
    factor = rows * n / (kvh * group * tq * n)
    imp_ref[...] = (jnp.sum(ibuf[...], axis=0) * factor).reshape(imp_ref.shape)

    column = jnp.bitwise_and(lanes, cap - 1)
    pos = jnp.bitwise_and(me - start_of, n - 1) + column * n
    slot = jnp.where(pos < count_of, lax.shift_right_logical(start_of + pos, shift), keep)
    keep_id = lax.broadcasted_iota(jnp.int32, (keep, rows), 0)
    place = jnp.where(keep_id == slot, 1.0, 0.0).astype(jnp.bfloat16)
    own_v.wait()

    @pl.loop(1, n)
    def _(d):
        s = lax.rem(me + d, n)
        arrived(picked.at[s], rbuf.at[s], v_s.at[d], v_r.at[s])

    kv_ref[...] = jnp.dot(
        place, rbuf[...].reshape(rows, proj.shape[1]), preferred_element_type=jnp.float32
    ).astype(jnp.bfloat16)

    @pl.loop(1, n)
    def _(d):
        c_copy(d).wait_send()
        v_copy(d).wait_send()

    for d in range(1, kvh):
        q_copy(d).wait_send()
        k_copy(d).wait_send()
        i_copy(d).wait_send()
    for d in range(1, planes):
        l_copy(d).wait_send()

    @pl.loop(0, planes)
    def _(t):
        relays(t, lambda c: c.wait_send())


def shards(queries, visual_keys, hidden, keep_count, keep_index, norm_gain, kv_weight, kv_bias):
    n = lax.axis_size("seq")
    kvh = visual_keys.shape[1] // HD
    rows, width = hidden.shape
    out_w = kv_weight.shape[1]
    tq = queries.shape[0]
    hw = queries.shape[1] // kvh
    nrow = hw // HD * tq
    cap = rows // n
    planes = n // kvh
    nch = kvh * rows // CH
    steps = width // KSTEP
    f32, bf16 = jnp.float32, jnp.bfloat16
    dma = pltpu.SemaphoreType.DMA
    hbm = pl.BlockSpec(memory_space=pl.ANY)
    vmem = pl.BlockSpec(memory_space=pltpu.VMEM)
    counts = jnp.broadcast_to(keep_count[:, None], (1, 128))
    importance, layer_kv = pl.pallas_call(
        functools.partial(body, n, kvh),
        out_shape=(
            jax.ShapeDtypeStruct((rows,), f32),
            jax.ShapeDtypeStruct((rows // 2, out_w), bf16),
        ),
        in_specs=[hbm, hbm, hbm, hbm, vmem, vmem, hbm, vmem],
        out_specs=(vmem, vmem),
        scratch_shapes=[
            pltpu.VMEM((planes, kvh, tq, hw), bf16),
            pltpu.VMEM((kvh, rows, HD), bf16),
            pltpu.VMEM((steps, rows, KSTEP), bf16),
            pltpu.VMEM((steps, KSTEP, out_w), bf16),
            pltpu.VMEM((n, 1, 128), jnp.int32),
            pltpu.VMEM((rows, 128), f32),
            pltpu.VMEM((rows, out_w), f32),
            pltpu.VMEM((rows, out_w), bf16),
            pltpu.VMEM((n, cap, out_w), bf16),
            pltpu.VMEM((n, cap, out_w), bf16),
            pltpu.VMEM((n, nch, CH, nrow), bf16),
            pltpu.VMEM((n, nch, nrow), f32),
            pltpu.VMEM((n, nch, nrow), f32),
            pltpu.VMEM((n, nrow), f32),
            pltpu.VMEM((planes, n, nrow), f32),
            pltpu.VMEM((kvh, 1, rows), f32),
            pltpu.VMEM((kvh, 1, rows), f32),
            pltpu.VMEM((rows, rows), bf16),
            dma((steps,)), dma((steps,)), dma((4,)),
            dma((kvh,)), dma((kvh,)), dma((kvh,)), dma((kvh,)),
            dma((n,)), dma((n,)), dma((n,)), dma((n,)),
            dma((planes,)), dma((planes,)), dma((kvh,)), dma((kvh,)),
            dma((planes,)), dma((planes,)), dma((planes,)),
        ],
        compiler_params=pltpu.CompilerParams(
            collective_id=0, has_side_effects=True, vmem_limit_bytes=66 * 1000 * 1000
        ),
    )(
        queries, visual_keys, hidden, counts, keep_index.reshape(1, rows),
        norm_gain.reshape(1, width), kv_weight, kv_bias.reshape(1, out_w),
    )
    return (importance, layer_kv)


def solution(mesh):
    placed = (
        P(("groups", "seq"), None),
        P(("groups", "seq"), None),
        P(("groups", "seq"), None),
        P(("groups", "seq")),
        P(("groups", "seq")),
        P(),
        P(),
        P(),
    )
    return jax.shard_map(
        shards,
        mesh=mesh,
        in_specs=placed,
        out_specs=(P(("groups", "seq")), P(("groups", "seq"), None)),
        check_vma=False,
    )
```
